512 devices in a mesh: seq: 16 (over z, core), dp: 8 (over y), mp: 4 (over x).
Axes of the slice: x: 4, y: 8, z: 8, core: 2. Of those that a mesh axis runs over, the one named last changes fastest.
Arguments:
- features: bfloat16 [8, 4096, 8, 512], P('dp', 'seq', None, 'mp'), may hold values from -6 to 6
- key_projection: bfloat16 [8, 4096, 8, 128], P('dp', 'seq'), may hold values from -2 to 2
- query_proj: bfloat16 [8, 4096, 8, 128], P('dp', 'seq'), may hold values from -2 to 2
- step_raw: float32 [8, 4096, 8, 8], P('dp', 'seq', None, 'mp'), may hold values from -3 to 6
- doc_starts: int32 [8, 4096], P('dp', 'seq'), may hold values 0 or 1
- log_rate: float32 [8, 8], P(None, 'mp'), may hold values from -5 to 1
- step_bias: float32 [8, 8], P(None, 'mp'), may hold values from -5 to -2.5
- skip_gain: float32 [8, 8], P(None, 'mp'), may hold values from 0.5 to 1.5
- out_grad: bfloat16 [8, 4096, 8, 512], P('dp', 'seq', None, 'mp'), may hold values from -6 to 6
Outputs:
- mixed_out: bfloat16 [8, 4096, 8, 512], P('dp', 'seq', None, 'mp')
- features_grad: bfloat16 [8, 4096, 8, 512], P('dp', 'seq', None, 'mp')
- key_grad: bfloat16 [8, 4096, 8, 128], P('dp', 'seq', 'mp')
- query_grad: bfloat16 [8, 4096, 8, 128], P('dp', 'seq', 'mp')
- step_grad: float32 [8, 4096, 8, 8], P('dp', 'seq', None, 'mp')
- log_rate_grad: float32 [8, 8], P(None, 'mp')
- step_bias_grad: float32 [8, 8], P(None, 'mp')
- skip_grad: float32 [8, 8], P(None, 'mp')
The draws below stay inside these ranges and needn't reach their ends.
All inputs are finite; a program needn't handle non-finite values. No bound on the sum of `doc_starts` on one device may be relied on, other than what follows from the above.
Results may differ from the reference program's by a relative error of at most 0.0015.
Values sent between devices are 32-bit elements; how exact they have to be, the bound alone decides.
No kernel may reach another device: no remote copies, remote signals or barrier semaphores. Data moves between devices by JAX's collectives and lax.ppermute only.
A program may use at most 128 MiB of HBM per device.

```python
import math
import jax
import jax.numpy as jnp
from jax import lax

G = 8
HG = 8
P_SIZE = 64
N = 128
TOK_DEV = 256
BATCH_LINES = 8
SPAN_TOKENS = 4096


def draw_step_raw(key, part):
    starting_seed, jump_seed_handle = jax.random.split(key)
    full_shape = (BATCH_LINES, SPAN_TOKENS, G, HG)
    starting_entries = jnp.clip(0.7 * jax.random.normal(starting_seed, full_shape, jnp.float32), -3.0, 3.0)
    sudden_jumps = jax.random.bernoulli(jump_seed_handle, 3.0 / SPAN_TOKENS, (BATCH_LINES, SPAN_TOKENS, 1, 1))
    return starting_entries + jnp.where(sudden_jumps, 3.0, 0.0)


def set_ends(entries, own_key, smallest, top_value):
    longest = entries.shape.index(max(entries.shape))
    spots = []
    for shift in (0, 1):
        where = [jax.random.randint(jax.random.fold_in(own_key, axis), (), 0, length) for axis, length in enumerate(entries.shape)]
        where[longest] = (where[longest] + shift) % entries.shape[longest]
        spots.append(tuple(where))
    return entries.at[spots[0]].set(smallest).at[spots[1]].set(top_value)


def level_of(stream_key, dims, shards, smallest, high):
    def one(dim, shards_of):
        steps = jax.random.uniform(jax.random.fold_in(jax.random.fold_in(stream_key, 6), dim), (shards_of,), jnp.float32, smallest / len(shards), high / len(shards))
        return jnp.repeat(jnp.exp(steps), dims[dim] // shards_of).reshape((-1,) + (1,) * (len(dims) - dim - 1))

    level = one(*shards[0])
    for cut in shards[1:]:
        level = level * one(*cut)
    return level


def bell_draw(own_key, dims, spread, reach, cuts=(), dtype=jnp.bfloat16):
    entries = jax.random.normal(own_key, dims, jnp.float32) * spread
    if len(cuts) > 0:
        entries = level_of(own_key, dims, cuts, -0.22, 0.18) * entries
    return jnp.clip(entries, min=-reach, max=reach).astype(dtype)


def setup_inputs(seed: int = 0) -> dict:
    streams_of = jax.random.split(jax.random.key(seed), 10)
    features = bell_draw(streams_of[0], (BATCH_LINES, SPAN_TOKENS, G, HG * P_SIZE), 1.0, 6.0, ((0, 8), (1, 16), (3, 4)))
    key_projection = bell_draw(streams_of[1], (BATCH_LINES, SPAN_TOKENS, G, N), 0.3, 2.0, ((0, 8), (1, 16)))
    query_proj = bell_draw(streams_of[2], (BATCH_LINES, SPAN_TOKENS, G, N), 0.3, 2.0, ((0, 8), (1, 16)))
    step_raw = draw_step_raw(jax.random.fold_in(streams_of[9], 71), 0)
    doc_starts = set_ends((jax.random.randint(streams_of[4], (BATCH_LINES, SPAN_TOKENS), 0, 3 * TOK_DEV) < 1).astype(jnp.int32), jax.random.fold_in(streams_of[4], 1), 0, 1)
    log_rate = jnp.clip(-5.0 + 6.0 * jax.random.uniform(streams_of[5], (G, HG), jnp.float32) ** level_of(streams_of[5], (G, HG), ((1, 4),), -0.2, 0.2), -5.0, 1.0)
    step_bias = jnp.clip(-5.0 + 2.5 * jax.random.uniform(streams_of[6], (G, HG), jnp.float32) ** level_of(streams_of[6], (G, HG), ((1, 4),), -0.2, 0.2), -5.0, -2.5)
    skip_gain = jnp.clip(0.5 + 1.0 * jax.random.uniform(streams_of[7], (G, HG), jnp.float32) ** level_of(streams_of[7], (G, HG), ((1, 4),), -0.2, 0.2), 0.5, 1.5)
    out_grad = bell_draw(streams_of[8], (BATCH_LINES, SPAN_TOKENS, G, HG * P_SIZE), 1.0, 6.0, ((0, 8), (1, 16), (3, 4)))
    return dict(features=features, key_projection=key_projection, query_proj=query_proj, step_raw=step_raw, doc_starts=doc_starts, log_rate=log_rate, step_bias=step_bias, skip_gain=skip_gain, out_grad=out_grad)


precise = lax.Precision.HIGHEST

def decay_terms(step_raw, doc_starts, log_rate, step_bias):
    step_size = jax.nn.softplus(step_raw + step_bias)
    log_decay = -step_size * jnp.exp(log_rate)
    cumulative = jnp.cumsum(log_decay, axis=1)
    doc_count = jnp.cumsum(doc_starts, axis=1)
    return (step_size, cumulative, doc_count)

def block_forward(head_vals, key_vals, query_vals, step_raw, doc_starts, log_rate, step_bias, skip_gain, state_in):
    step_size, cumulative, doc_count = decay_terms(step_raw, doc_starts, log_rate, step_bias)
    block_len = head_vals.shape[1]
    causal = jnp.arange(block_len)[:, None] >= jnp.arange(block_len)[None, :]
    same_doc = causal[None] & (doc_count[:, :, None] == doc_count[:, None, :])
    doc_mask = same_doc[..., None, None]
    gap_log = cumulative[:, :, None] - cumulative[:, None, :]
    decay_mat = jnp.where(doc_mask, jnp.exp(jnp.where(doc_mask, gap_log, 0.0)), 0.0)
    entry_decay = jnp.where((doc_count == 0)[:, :, None, None], jnp.exp(cumulative), 0.0)
    scores = jnp.einsum('rtgn,rsgn->rtsg', query_vals, key_vals, precision=precise)
    mixing = scores[..., None] * decay_mat * step_size[:, None]
    output = jnp.einsum('rtsgh,rsghp->rtghp', mixing, head_vals, precision=precise)
    output = output + jnp.einsum('rtgn,rghpn->rtghp', query_vals, state_in, precision=precise) * entry_decay[..., None]
    output = output + skip_gain[..., None] * head_vals
    last_decay = decay_mat[:, -1]
    state_out = state_in * entry_decay[:, -1][..., None, None]
    state_out = state_out + jnp.einsum('rsgh,rsghp,rsgn->rghpn', last_decay * step_size, head_vals, key_vals, precision=precise)
    return (output, state_out)

def reference(features, key_projection, query_proj, step_raw, doc_starts, log_rate, step_bias, skip_gain, out_grad):
    row_count, length, groups, feat_width = features.shape
    head_count = feat_width // P_SIZE
    block_len = math.gcd(length, 128)
    block_count = length // block_len
    head_vals = features.astype(jnp.float32).reshape(row_count, length, groups, head_count, P_SIZE)
    key_vals = key_projection.astype(jnp.float32)
    query_vals = query_proj.astype(jnp.float32)

    def to_blocks(array):
        return jnp.moveaxis(array.reshape((row_count, block_count, block_len) + array.shape[2:]), 1, 0)

    def forward(head_vals, key_vals, query_vals, step_raw, log_rate, step_bias, skip_gain):

        def stepper(state, pieces):
            vals_b, keys_b, queries_b, raw_b, starts_b = pieces
            output, new_state = block_forward(vals_b, keys_b, queries_b, raw_b, starts_b, log_rate, step_bias, skip_gain, state)
            return (new_state, output)
        zero_state = jnp.zeros((row_count, groups, head_count, P_SIZE, N), jnp.float32)
        _, block_outs = lax.scan(jax.checkpoint(stepper), zero_state, (to_blocks(head_vals), to_blocks(key_vals), to_blocks(query_vals), to_blocks(step_raw), to_blocks(doc_starts)))
        return jnp.moveaxis(block_outs, 0, 1).reshape(row_count, length, groups, head_count, P_SIZE)
    mixed_vals, pullback = jax.vjp(forward, head_vals, key_vals, query_vals, step_raw, log_rate, step_bias, skip_gain)
    cotangent = out_grad.astype(jnp.float32).reshape(head_vals.shape)
    vals_grad, keys_grad, queries_grad, raw_grad, rate_grad, bias_grad, gain_grad = pullback(cotangent)
    return (mixed_vals.reshape(features.shape).astype(jnp.bfloat16), vals_grad.reshape(features.shape).astype(jnp.bfloat16), keys_grad.astype(jnp.bfloat16), queries_grad.astype(jnp.bfloat16), raw_grad, rate_grad, bias_grad, gain_grad)
```

```python
import functools

import jax
import jax.numpy as jnp
from jax import lax
from jax.experimental import pallas as pl
from jax.experimental.pallas import tpu as pltpu
from jax.sharding import PartitionSpec as P


P_SIZE = 64
N = 128
F32 = jnp.float32
BF16 = jnp.bfloat16
NN = (((1,), (0,)), ((), ()))
NT = (((1,), (1,)), ((), ()))
TN = (((0,), (0,)), ((), ()))


def dot(a, b, dims=NN):
    return lax.dot_general(a, b, dims, preferred_element_type=F32)


def split(a):
    high = a.astype(BF16)
    return high, (a - high.astype(F32)).astype(BF16)


def exact_dot(a, b):
    return lax.dot_general(
        a, b, NN, precision=lax.Precision.HIGHEST, preferred_element_type=F32
    )


def softplus(v):
    u = jnp.exp(-jnp.abs(v))
    series = u * (1.0 + u * (-1.0 / 2 + u * (1.0 / 3 + u * (-1.0 / 4 + u * (1.0 / 5)))))
    return jnp.maximum(v, 0.0) + jnp.where(u < 0.03, series, jnp.log(1.0 + u))


def pair_rows(ref, pairs, length):
    rows = [jnp.full((1, length), ref[j % 2, j // 2], F32) for j in range(pairs)]
    return jnp.concatenate(rows, axis=0)


def two_heads(rows_ref, base, g, length):
    top = rows_ref[pl.ds(base + 2 * g, 1), :]
    low = rows_ref[pl.ds(base + 2 * g + 1, 1), :]
    return jnp.concatenate(
        [jnp.broadcast_to(top, (P_SIZE, length)), jnp.broadcast_to(low, (P_SIZE, length))], axis=0
    )


CUM, DT, ENTRY, TAIL, SIG, LOGD, DOC = 0, 16, 32, 48, 64, 80, 96
ROWS = 104


def summary_kernel(
    x_hbm, dy_hbm, b_hbm, c_hbm, raw_hbm, doc_hbm, rate_hbm, bias_hbm,
    keep_ref, give_ref, rows_ref,
    xs, ys, bs, cs, x_in, dy_in, b_in, c_in, raw_ref, doc_ref, rate_ref, bias_ref, sems,
):
    length, groups, _ = x_hbm.shape
    loads = [
        pltpu.make_async_copy(src, dst, sems.at[k])
        for k, (src, dst) in enumerate((
            (raw_hbm, raw_ref), (doc_hbm, doc_ref), (rate_hbm, rate_ref), (bias_hbm, bias_ref),
            (x_hbm, x_in), (dy_hbm, dy_in), (b_hbm, b_in), (c_hbm, c_in),
        ))
    ]
    for load in loads:
        load.start()
    for load in loads[:4]:
        load.wait()
    pairs = 2 * groups
    core = core_of_chip()
    raw = jnp.concatenate([raw_ref[g] for g in range(groups)], axis=0)
    shifted = raw + pair_rows(bias_ref, pairs, length)
    dt = softplus(shifted)
    log_decay = -dt * jnp.exp(pair_rows(rate_ref, pairs, length))
    docs = jnp.broadcast_to(doc_ref[...].astype(F32), (8, length))
    before = lax.broadcasted_iota(jnp.int32, (length, length), 0)
    after = lax.broadcasted_iota(jnp.int32, (length, length), 1)
    upto = jnp.where(before <= after, 1.0, 0.0).astype(F32)
    sums = exact_dot(jnp.concatenate([log_decay, docs], axis=0), upto)
    cum = sums[:pairs]
    count = sums[pairs : pairs + 1]
    last = cum[:, length - 1 :]
    last_count = count[:, length - 1 :]
    entry = jnp.where(count == 0.0, jnp.exp(cum), 0.0)
    tail = jnp.where(count == last_count, jnp.exp(last - cum), 0.0) * dt
    rows_ref[CUM : CUM + 16] = cum
    rows_ref[DT : DT + 16] = dt
    rows_ref[ENTRY : ENTRY + 16] = entry
    rows_ref[TAIL : TAIL + 16] = tail
    rows_ref[SIG : SIG + 16] = 1.0 / (1.0 + jnp.exp(-shifted))
    rows_ref[LOGD : LOGD + 16] = log_decay
    rows_ref[DOC : DOC + 8] = jnp.broadcast_to(count, (8, length))
    for load, src, dst in zip(loads[4:], (x_in, dy_in, b_in, c_in), (xs, ys, bs, cs)):
        load.wait()
        dst[...] = src[...].astype(F32).reshape(length * groups, 128)

    def group(g, carry):
        x_t = xs[pl.ds(g, length, stride=groups), :].T
        dy_t = ys[pl.ds(g, length, stride=groups), :].T
        b_n = bs[pl.ds(g, length, stride=groups), :].astype(BF16)
        c_n = cs[pl.ds(g, length, stride=groups), :].astype(BF16)
        totals = []
        for vals, weights, other in ((x_t, TAIL, b_n), (dy_t, ENTRY, c_n)):
            high, low = split(vals * two_heads(rows_ref, weights, g, length))
            both = dot(jnp.concatenate([high, low], axis=0), other)
            totals.append(both[:128] + both[128:])

        def store(ref):
            for h in range(2):
                slot = 2 * lax.rem(g, groups // 2) + h
                passed = rows_ref[pl.ds(ENTRY + 2 * g + h, 1), :][:, length - 1 :]
                for at, total in zip((0, P_SIZE), totals):
                    ref[slot, at : at + P_SIZE] = total[h * P_SIZE : (h + 1) * P_SIZE]
                ref[slot, 2 * P_SIZE :] = jnp.broadcast_to(passed, (8, N))

        mine = g // (groups // 2) == core
        pl.when(mine)(lambda: store(keep_ref))
        pl.when(jnp.logical_not(mine))(lambda: store(give_ref))
        return carry

    lax.fori_loop(0, groups, group, 0)


def core_of_chip():
    return lax.rem(lax.axis_index("seq"), 2)


def state_of(ref, k):
    return ref[k, :P_SIZE]


def adjoint_of(ref, k):
    return ref[k, P_SIZE : 2 * P_SIZE]


def passed_of(ref, k):
    return ref[k, 2 * P_SIZE : 2 * P_SIZE + 1, :]


def chip_kernel(keep_ref, got_ref, chip_ref):
    def join(first, second):
        for k in range(chip_ref.shape[0]):
            chip_ref[k, :P_SIZE] = passed_of(second, k) * state_of(first, k) + state_of(second, k)
            chip_ref[k, P_SIZE : 2 * P_SIZE] = adjoint_of(first, k) + passed_of(
                first, k
            ) * adjoint_of(second, k)
            chip_ref[k, 2 * P_SIZE :] = first[k, 2 * P_SIZE :] * second[k, 2 * P_SIZE :]

    core = core_of_chip()
    pl.when(core == 0)(lambda: join(keep_ref, got_ref))
    pl.when(core == 1)(lambda: join(got_ref, keep_ref))


def scan_kernel(recv_ref, send_ref):
    chips = recv_ref.shape[0]
    state = jnp.zeros((P_SIZE, N), F32)
    for k in range(chips):
        send_ref[k, :P_SIZE] = state
        if k < chips - 1:
            state = passed_of(recv_ref, k) * state + state_of(recv_ref, k)
    state = jnp.zeros((P_SIZE, N), F32)
    for k in reversed(range(chips)):
        send_ref[k, P_SIZE:] = state
        if k > 0:
            state = passed_of(recv_ref, k) * state + adjoint_of(recv_ref, k)


def shard_kernel(keep_ref, got_ref, chip_ref, mine_ref, theirs_ref):
    def part(first, second, first_out, second_out):
        for k in range(chip_ref.shape[0]):
            state, adjoint = chip_ref[k, :P_SIZE], chip_ref[k, P_SIZE:]
            first_out[k, :P_SIZE] = state
            first_out[k, P_SIZE:] = passed_of(second, k) * adjoint + adjoint_of(second, k)
            second_out[k, :P_SIZE] = passed_of(first, k) * state + state_of(first, k)
            second_out[k, P_SIZE:] = adjoint

    core = core_of_chip()
    pl.when(core == 0)(lambda: part(keep_ref, got_ref, mine_ref, theirs_ref))
    pl.when(core == 1)(lambda: part(got_ref, keep_ref, theirs_ref, mine_ref))


def states_of(mine_ref, other_ref, g, groups, at):
    mine = g // (groups // 2) == core_of_chip()
    slot = 2 * lax.rem(g, groups // 2)
    return [
        jnp.where(mine, mine_ref[slot + h, at : at + P_SIZE], other_ref[slot + h, at : at + P_SIZE])
        for h in range(2)
    ]


def within_kernel(
    start,
    x_ref, dy_ref, b_ref, c_ref, rows_ref,
    yt_ref, dxt_ref, dct_ref, dbt_ref, xt_ref, dyt_ref, bt_ref, ct_ref,
    xs, ys, bs, cs,
):
    groups, _, length = yt_ref.shape
    stride = x_ref.shape[1]
    for src, dst in ((x_ref, xs), (dy_ref, ys), (b_ref, bs), (c_ref, cs)):
        dst[...] = src[...].astype(F32).reshape(length * stride, 128)
    t_at = lax.broadcasted_iota(jnp.int32, (length, length), 0)
    s_at = lax.broadcasted_iota(jnp.int32, (length, length), 1)
    count = rows_ref[DOC : DOC + 8]
    count_col = count.T[:, :1]
    far = jnp.where((t_at >= s_at) & (count_col == count[:1]), 0.0, -jnp.inf)
    lanes = lax.broadcasted_iota(jnp.int32, (length, 128), 1)

    def group(i, carry):
        g = start + i
        x_n, dy_n, b_n, c_n = (
            ref[pl.ds(g, length, stride=stride), :] for ref in (xs, ys, bs, cs)
        )
        b_t, c_t = b_n.T.astype(BF16), c_n.T.astype(BF16)
        c_n, dy_n, x_t = c_n.astype(BF16), dy_n.astype(BF16), x_n.T.astype(BF16)
        bt_ref[i] = b_t
        ct_ref[i] = c_t
        xt_ref[i] = x_t
        dyt_ref[i] = dy_n.T
        scores = dot(c_n, b_t)
        cum = jnp.concatenate(
            [rows_ref[pl.ds(CUM + 2 * g, 1), :], rows_ref[pl.ds(CUM + 2 * g + 1, 1), :]]
            + [jnp.zeros((6, length), F32)],
            axis=0,
        )
        cum_col = cum.T
        score_grad = None
        for h in range(2):
            part = slice(h * P_SIZE, (h + 1) * P_SIZE)
            dt = rows_ref[pl.ds(DT + 2 * g + h, 1), :]
            weight = jnp.exp(cum_col[:, h : h + 1] - cum[h : h + 1] + far) * dt
            high, low = split(scores * weight)
            x_h = xt_ref[i, part, :]
            dy_h = dyt_ref[i, part, :]
            yt_ref[i, part, :] = dot(x_h, high, NT) + dot(x_h, low, NT)
            dxt_ref[i, part, :] = dot(dy_h, high) + dot(dy_h, low)
            mine = (lanes < P_SIZE) if h == 0 else (lanes >= P_SIZE)
            mixing_grad = dot(jnp.where(mine, dy_n, jnp.zeros_like(dy_n)), x_t)
            score_grad = mixing_grad * weight if h == 0 else score_grad + mixing_grad * weight
        high, low = split(score_grad)
        dct_ref[i] = dot(b_t, high, NT) + dot(b_t, low, NT)
        dbt_ref[i] = dot(c_t, high) + dot(c_t, low)
        return carry

    lax.fori_loop(0, groups, group, 0)


def group_grad_kernel(
    mine_ref, other_ref, rows_ref,
    xt0_ref, xt1_ref, dyt0_ref, dyt1_ref, dct0_ref, dct1_ref, dbt0_ref, dbt1_ref,
    *send_refs,
):
    groups, _, _ = xt0_ref.shape
    groups *= 2
    owned = groups // len(send_refs)
    me = lax.axis_index("mp")

    def group(start, bases, i, carry):
        g = start + i
        totals = []
        for at, vals_ref, weights, base_ref in (
            (0, bases[0], ENTRY, bases[1]),
            (P_SIZE, bases[2], TAIL, bases[3]),
        ):
            total = base_ref[i]
            for h, state in enumerate(states_of(mine_ref, other_ref, g, groups, at)):
                high, low = split(state)
                vals = vals_ref[i, h * P_SIZE : (h + 1) * P_SIZE, :]
                grad = dot(
                    jnp.concatenate([high, low], axis=0),
                    jnp.concatenate([vals, vals], axis=0),
                    TN,
                )
                total = total + grad * rows_ref[pl.ds(weights + 2 * g + h, 1), :]
            totals.append(total)

        def store(ref):
            for which, total in enumerate(totals):
                ref[2 * lax.rem(g, owned) + which] = total

        away = lax.bitwise_xor(g // owned, me)
        for k, ref in enumerate(send_refs):
            pl.when(away == k)(functools.partial(store, ref))
        return carry

    half = groups // 2
    lax.fori_loop(0, half, functools.partial(group, 0, (dyt0_ref, dct0_ref, xt0_ref, dbt0_ref)), 0)
    lax.fori_loop(0, half, functools.partial(group, half, (dyt1_ref, dct1_ref, xt1_ref, dbt1_ref)), 0)


def finish_kernel(
    mine_ref, other_ref, rows_ref, xt0_ref, xt1_ref, dyt0_ref, dyt1_ref,
    bt0_ref, bt1_ref, ct0_ref, ct1_ref, yt0_ref, yt1_ref, dxt0_ref, dxt1_ref,
    rate_ref, gain_ref, order_ref,
    out_ref, dx_ref, raw_grad_ref, stats_ref,
    ys, dxs, through, back, skip, bound,
):
    groups, _, length = xt0_ref.shape
    groups *= 2
    pairs = 2 * groups
    both_heads = lax.broadcasted_iota(jnp.int32, (128, length), 0) < P_SIZE

    def group(start, bases, i, carry):
        g = start + i
        xt_ref, dyt_ref, bt_ref, ct_ref, yt_ref, dxt_ref = bases
        x_t, dy_t = xt_ref[i].astype(F32), dyt_ref[i].astype(F32)
        states = states_of(mine_ref, other_ref, g, groups, 0)
        adjoints = states_of(mine_ref, other_ref, g, groups, P_SIZE)

        def entering(state, other):
            high, low = split(jnp.concatenate(state, axis=0))
            return dot(
                jnp.concatenate([high, low], axis=1), jnp.concatenate([other, other], axis=0)
            )

        y_t = yt_ref[i] + entering(states, ct_ref[i]) * two_heads(rows_ref, ENTRY, g, length)
        dx_far = entering(adjoints, bt_ref[i]) * two_heads(rows_ref, TAIL, g, length)
        dx_t = dxt_ref[i] + dx_far
        gain = jnp.where(both_heads, gain_ref[0, g], gain_ref[1, g])
        ys[pl.ds(g, length, stride=groups), :] = (y_t + gain * x_t).T
        dxs[pl.ds(g, length, stride=groups), :] = (dx_t + gain * dy_t).T
        forward, backward = dy_t * y_t, x_t * dx_t
        direct, far = dy_t * x_t, x_t * dx_far
        for h in range(2):
            part = slice(h * P_SIZE, (h + 1) * P_SIZE)
            at = pl.ds(2 * g + h, 1)
            through[at, :] = jnp.sum(forward[part], axis=0, keepdims=True)
            back[at, :] = jnp.sum(backward[part], axis=0, keepdims=True)
            skip[at, :] = jnp.sum(direct[part], axis=0, keepdims=True)
            meet = jnp.sum(states[h] * adjoints[h], axis=0, keepdims=True)
            passed = rows_ref[pl.ds(ENTRY + 2 * g + h, 1), :][:, length - 1 :]
            arrive = jnp.sum(far[part], axis=0, keepdims=True)
            bound[at, :] = arrive + jnp.concatenate(
                [meet * passed, jnp.zeros((1, length - N), F32)], axis=1
            )
        return carry

    half = groups // 2
    first = (xt0_ref, dyt0_ref, bt0_ref, ct0_ref, yt0_ref, dxt0_ref)
    second = (xt1_ref, dyt1_ref, bt1_ref, ct1_ref, yt1_ref, dxt1_ref)
    lax.fori_loop(0, half, functools.partial(group, 0, first), 0)
    lax.fori_loop(0, half, functools.partial(group, half, second), 0)
    out_ref[...] = ys[...].reshape(length, groups, 128).astype(BF16)
    dx_ref[...] = dxs[...].reshape(length, groups, 128).astype(BF16)

    dt = rows_ref[DT : DT + 16]
    rate = jnp.exp(pair_rows(rate_ref, pairs, length))
    before = lax.broadcasted_iota(jnp.int32, (length, length), 0)
    after = lax.broadcasted_iota(jnp.int32, (length, length), 1)
    since = jnp.where(before >= after, 1.0, 0.0).astype(F32)
    decay_grad = exact_dot(through[...] - back[...], since)
    decay_grad = decay_grad + jnp.sum(bound[...], axis=1, keepdims=True)
    raw_grad = (back[...] / dt - rate * decay_grad) * rows_ref[SIG : SIG + 16]
    for g in range(groups):
        raw_grad_ref[g] = raw_grad[2 * g : 2 * g + 2]
    rate_grad = jnp.sum(decay_grad * rows_ref[LOGD : LOGD + 16], axis=1, keepdims=True)
    bias_grad = jnp.sum(raw_grad, axis=1, keepdims=True)
    gain_grad = jnp.sum(skip[...], axis=1, keepdims=True)
    lane = lax.broadcasted_iota(jnp.int32, (pairs, 128), 1)
    stats_ref[...] = jnp.where(
        lane == 0, rate_grad, jnp.where(lane == 1, bias_grad, jnp.where(lane == 2, gain_grad, 0.0))
    )


def gather_kernel(*refs):
    parts, (key_ref, query_ref, keys, queries) = refs[:-4], refs[-4:]
    slots, _, length = parts[0].shape
    for slot in range(slots):
        total = parts[0][slot]
        for part in parts[1:]:
            total = total + part[slot]
        dst = keys if slot % 2 else queries
        dst[pl.ds(slot // 2, length, stride=slots // 2), :] = total.T
    key_ref[...] = keys[...].reshape(key_ref.shape).astype(BF16)
    query_ref[...] = queries[...].reshape(query_ref.shape).astype(BF16)


def call(kernel, out, scratch=(), smem=(), hbm=(), flops=10**9, moved=4 << 20, vmem=24):
    def run(*args):
        spaces = [
            pltpu.SMEM if i in smem else pltpu.HBM if i in hbm else pltpu.VMEM
            for i in range(len(args))
        ]
        return pl.pallas_call(
            kernel,
            out_shape=out,
            in_specs=[pl.BlockSpec(memory_space=space) for space in spaces],
            out_specs=jax.tree.map(lambda _: pl.BlockSpec(memory_space=pltpu.VMEM), out),
            scratch_shapes=list(scratch),
            cost_estimate=pl.CostEstimate(flops=flops, bytes_accessed=moved, transcendentals=0),
            compiler_params=pltpu.CompilerParams(vmem_limit_bytes=vmem << 20),
        )(*args)

    return run


def local(
    features, key_projection, query_proj, step_raw, doc_starts, log_rate, step_bias, skip_gain,
    out_grad,
):
    _, length, groups, _ = features.shape
    pairs = 2 * groups
    half = groups // 2
    shards, owners = lax.axis_size("seq"), lax.axis_size("mp")
    shape = jax.ShapeDtypeStruct
    flat = pltpu.VMEM((length * groups, 128), F32)
    half_full = shape((half, 128, length), F32)
    half_wide = shape((half, 128, length), BF16)
    per_pair = pltpu.VMEM((pairs, length), F32)
    summary = shape((groups, 2 * P_SIZE + 8, N), F32)
    entering = shape((groups, 2 * P_SIZE, N), F32)
    rate, bias, gain = log_rate.T, step_bias.T, skip_gain.T
    partner = [(i, i ^ 1) for i in range(shards)]
    cores = [list(range(c, shards, 2)) for c in range(2)]

    def to_chips(a):
        return lax.all_to_all(a, "seq", 0, 0, axis_index_groups=cores, tiled=True)

    keep, give, rows = call(
        summary_kernel,
        (summary, summary, shape((ROWS, length), F32)),
        scratch=[flat] * 4 + [pltpu.VMEM((length, groups, 128), BF16)] * 4
        + [pltpu.VMEM((groups, 2, length), F32), pltpu.VMEM((1, length), jnp.int32)]
        + [pltpu.SMEM((2, groups), F32)] * 2 + [pltpu.SemaphoreType.DMA((8,))],
        hbm=range(8), vmem=62,
    )(features[0], out_grad[0], key_projection[0], query_proj[0],
      step_raw[0].transpose(1, 2, 0), doc_starts, rate, bias)
    got = lax.ppermute(give, "seq", partner)
    chip = call(chip_kernel, summary, vmem=60)(keep, got)
    scanned = call(scan_kernel, entering)(to_chips(chip))
    ends = to_chips(scanned)
    mine, theirs = call(shard_kernel, (entering, entering), vmem=60)(keep, got, ends)
    other = lax.ppermute(theirs, "seq", partner)
    within = [
        call(
            functools.partial(within_kernel, start),
            (half_full,) * 4 + (half_wide,) * 4, scratch=[flat] * 4, flops=10**10, vmem=60,
        )(features[0], out_grad[0], key_projection[0], query_proj[0], rows)
        for start in (0, half)
    ]
    y_in, dx_in, dc_in, db_in, x_t, dy_t, b_t, c_t = zip(*within)
    owned = groups // owners
    part = shape((2 * owned, 128, length), F32)
    grads = call(group_grad_kernel, (part,) * owners)(
        mine, other, rows, *x_t, *dy_t, *dc_in, *db_in
    )
    parts = [grads[0]]
    for k in range(1, owners):
        parts.append(lax.ppermute(grads[k], "mp", [(i, i ^ k) for i in range(owners)]))
    mixed, dx, raw_grad, stats = call(
        finish_kernel,
        (shape((length, groups, 128), BF16), shape((length, groups, 128), BF16),
         shape((groups, 2, length), F32), shape((pairs, 128), F32)),
        scratch=[flat, flat, per_pair, per_pair, per_pair, per_pair],
        smem=(15, 16), hbm=(17,), vmem=60,
    )(mine, other, rows, *x_t, *dy_t, *b_t, *c_t, *y_in, *dx_in, rate, gain, grads[0])
    stats = stats[:, :3]
    for axis in ("seq", "dp"):
        copies = jnp.broadcast_to(stats, (lax.axis_size(axis),) + stats.shape)
        copies = lax.all_to_all(copies, axis, 0, 0, tiled=True)
        stats = jnp.sum(copies, axis=0)
    out_grads = shape((length, owned, 128), BF16)
    key_grad, query_grad = call(
        gather_kernel, (out_grads, out_grads),
        scratch=[pltpu.VMEM((length * owned, 128), F32)] * 2,
    )(*parts)
    stats = stats.reshape(groups, 2, 3)
    return (
        mixed[None],
        dx[None],
        key_grad[None],
        query_grad[None],
        raw_grad.transpose(2, 0, 1)[None],
        stats[..., 0],
        stats[..., 1],
        stats[..., 2],
    )


def solution(mesh):
    return jax.shard_map(
        local,
        mesh=mesh,
        in_specs=(
            P("dp", "seq", None, "mp"),
            P("dp", "seq", None, None),
            P("dp", "seq", None, None),
            P("dp", "seq", None, "mp"),
            P("dp", "seq"),
            P(None, "mp"),
            P(None, "mp"),
            P(None, "mp"),
            P("dp", "seq", None, "mp"),
        ),
        out_specs=(
            P("dp", "seq", None, "mp"),
            P("dp", "seq", None, "mp"),
            P("dp", "seq", "mp", None),
            P("dp", "seq", "mp", None),
            P("dp", "seq", None, "mp"),
            P(None, "mp"),
            P(None, "mp"),
            P(None, "mp"),
        ),
        check_vma=False,
    )
```

```python
import functools

import jax
import jax.numpy as jnp
from jax import lax
from jax.experimental import pallas as pl
from jax.experimental.pallas import tpu as pltpu
from jax.sharding import PartitionSpec as P


P_SIZE = 64
N = 128
F32 = jnp.float32
BF16 = jnp.bfloat16
NN = (((1,), (0,)), ((), ()))
NT = (((1,), (1,)), ((), ()))
TN = (((0,), (0,)), ((), ()))


def dot(a, b, dims=NN):
    return lax.dot_general(a, b, dims, preferred_element_type=F32)


def split(a):
    high = a.astype(BF16)
    return high, (a - high.astype(F32)).astype(BF16)


def exact_dot(a, b):
    return lax.dot_general(
        a, b, NN, precision=lax.Precision.HIGHEST, preferred_element_type=F32
    )


def softplus(v):
    u = jnp.exp(-jnp.abs(v))
    series = u * (1.0 + u * (-1.0 / 2 + u * (1.0 / 3 + u * (-1.0 / 4 + u * (1.0 / 5)))))
    return jnp.maximum(v, 0.0) + jnp.where(u < 0.03, series, jnp.log(1.0 + u))


def pair_rows(ref, pairs, length):
    half = pairs // 2
    rows = [jnp.full((1, length), ref[j // half, j % half], F32) for j in range(pairs)]
    return jnp.concatenate(rows, axis=0)


def row_of(base, g, h):
    return pl.ds(base + 8 * h + g, 1)


def two_heads(rows_ref, base, g, length):
    top, low = rows_ref[row_of(base, g, 0), :], rows_ref[row_of(base, g, 1), :]
    return jnp.concatenate(
        [jnp.broadcast_to(top, (P_SIZE, length)), jnp.broadcast_to(low, (P_SIZE, length))], axis=0
    )


CUM, DT, ENTRY, TAIL, SIG, LOGD, DOC = 0, 16, 32, 48, 64, 80, 96
ROWS = 104


def summary_kernel(
    x_hbm, dy_hbm, b_hbm, c_hbm, raw_hbm, doc_hbm, rate_hbm, bias_hbm,
    keep_ref, give_ref, rows_ref,
    xs, ys, bs, cs, x_in, dy_in, b_in, c_in, raw_ref, doc_ref, rate_ref, bias_ref, sems,
):
    length, groups, _ = x_hbm.shape
    loads = [
        pltpu.make_async_copy(src, dst, sems.at[k])
        for k, (src, dst) in enumerate((
            (raw_hbm, raw_ref), (doc_hbm, doc_ref), (rate_hbm, rate_ref), (bias_hbm, bias_ref),
            (x_hbm, x_in), (dy_hbm, dy_in), (b_hbm, b_in), (c_hbm, c_in),
        ))
    ]
    for load in loads:
        load.start()
    for load in loads[:4]:
        load.wait()
    pairs = 2 * groups
    core = core_of_chip()
    raw = jnp.concatenate(
        [raw_ref[g, h : h + 1, :] for h in range(2) for g in range(groups)], axis=0
    )
    shifted = raw + pair_rows(bias_ref, pairs, length)
    dt = softplus(shifted)
    log_decay = -dt * jnp.exp(pair_rows(rate_ref, pairs, length))
    docs = jnp.broadcast_to(doc_ref[...].astype(F32), (8, length))
    before = lax.broadcasted_iota(jnp.int32, (length, length), 0)
    after = lax.broadcasted_iota(jnp.int32, (length, length), 1)
    upto = jnp.where(before <= after, 1.0, 0.0).astype(F32)
    sums = exact_dot(jnp.concatenate([log_decay, docs], axis=0), upto)
    cum = sums[:pairs]
    count = sums[pairs : pairs + 1]
    last = cum[:, length - 1 :]
    last_count = count[:, length - 1 :]
    entry = jnp.where(count == 0.0, jnp.exp(cum), 0.0)
    tail = jnp.where(count == last_count, jnp.exp(last - cum), 0.0) * dt
    rows_ref[CUM : CUM + 16] = cum
    rows_ref[DT : DT + 16] = dt
    rows_ref[ENTRY : ENTRY + 16] = entry
    rows_ref[TAIL : TAIL + 16] = tail
    rows_ref[SIG : SIG + 16] = 1.0 / (1.0 + jnp.exp(-shifted))
    rows_ref[LOGD : LOGD + 16] = log_decay
    rows_ref[DOC : DOC + 8] = jnp.broadcast_to(count, (8, length))
    for load, src, dst in zip(loads[4:], (x_in, dy_in, b_in, c_in), (xs, ys, bs, cs)):
        load.wait()
        dst[...] = src[...].astype(F32).reshape(length * groups, 128)

    def totals_of(g):
        x_t = xs[pl.ds(g, length, stride=groups), :].T
        dy_t = ys[pl.ds(g, length, stride=groups), :].T
        b_n = bs[pl.ds(g, length, stride=groups), :].astype(BF16)
        c_n = cs[pl.ds(g, length, stride=groups), :].astype(BF16)
        totals = []
        for vals, weights, other in ((x_t, TAIL, b_n), (dy_t, ENTRY, c_n)):
            high, low = split(vals * two_heads(rows_ref, weights, g, length))
            both = dot(jnp.concatenate([high, low], axis=0), other)
            totals.append(both[:128] + both[128:])
        return totals

    half = groups // 2
    passed = entry[:, length - 1 :]
    for i in range(half):
        low, high = totals_of(i), totals_of(half + i)
        for h in range(2):
            part = slice(h * P_SIZE, (h + 1) * P_SIZE)
            for at, a, b in zip((0, P_SIZE), low, high):
                keep_ref[2 * i + h, at : at + P_SIZE] = jnp.where(core == 0, a[part], b[part])
                give_ref[2 * i + h, at : at + P_SIZE] = jnp.where(core == 0, b[part], a[part])
            a = jnp.broadcast_to(passed[groups * h + i : groups * h + i + 1], (8, N))
            b = jnp.broadcast_to(passed[groups * h + half + i : groups * h + half + i + 1], (8, N))
            keep_ref[2 * i + h, 2 * P_SIZE :] = jnp.where(core == 0, a, b)
            give_ref[2 * i + h, 2 * P_SIZE :] = jnp.where(core == 0, b, a)


def core_of_chip():
    return lax.rem(lax.axis_index("seq"), 2)


def state_of(ref, k):
    return ref[k, :P_SIZE]


def adjoint_of(ref, k):
    return ref[k, P_SIZE : 2 * P_SIZE]


def passed_of(ref, k):
    return ref[k, 2 * P_SIZE : 2 * P_SIZE + 1, :]


def chip_kernel(keep_ref, got_ref, chip_ref):
    def join(first, second):
        for k in range(chip_ref.shape[0]):
            chip_ref[k, :P_SIZE] = passed_of(second, k) * state_of(first, k) + state_of(second, k)
            chip_ref[k, P_SIZE : 2 * P_SIZE] = adjoint_of(first, k) + passed_of(
                first, k
            ) * adjoint_of(second, k)
            chip_ref[k, 2 * P_SIZE :] = first[k, 2 * P_SIZE :] * second[k, 2 * P_SIZE :]

    core = core_of_chip()
    pl.when(core == 0)(lambda: join(keep_ref, got_ref))
    pl.when(core == 1)(lambda: join(got_ref, keep_ref))


def scan_kernel(recv_ref, send_ref):
    chips = recv_ref.shape[0]
    state = jnp.zeros((P_SIZE, N), F32)
    for k in range(chips):
        send_ref[k, :P_SIZE] = state
        if k < chips - 1:
            state = passed_of(recv_ref, k) * state + state_of(recv_ref, k)
    state = jnp.zeros((P_SIZE, N), F32)
    for k in reversed(range(chips)):
        send_ref[k, P_SIZE:] = state
        if k > 0:
            state = passed_of(recv_ref, k) * state + adjoint_of(recv_ref, k)


def states_of(refs, g, groups, at):
    core = core_of_chip()
    mine = g // (groups // 2) == core
    through = core == (1 if at == 0 else 0)
    slot = 2 * lax.rem(g, groups // 2)
    ends_mine, ends_other, sums_mine, sums_other = refs
    part = slice(at, at + P_SIZE)
    states = []
    for k in (slot, slot + 1):
        end = jnp.where(mine, ends_mine[k, part], ends_other[k, part])
        summary = jnp.where(mine, sums_mine[k, part], sums_other[k, part])
        passed = jnp.where(mine, passed_of(sums_mine, k), passed_of(sums_other, k))
        states.append(jnp.where(through, passed * end + summary, end))
    return states


def within_kernel(
    start,
    x_ref, dy_ref, b_ref, c_ref, rows_ref,
    *rest,
):
    yt_ref, dxt_ref, dct_ref, dbt_ref, xt_ref, dyt_ref, bt_ref, ct_ref, xs, ys, bs, cs = rest[-12:]
    groups, _, length = yt_ref.shape
    stride = x_ref.shape[1]
    for src, dst in ((x_ref, xs), (dy_ref, ys), (b_ref, bs), (c_ref, cs)):
        dst[...] = src[...].astype(F32).reshape(length * stride, 128)
    t_at = lax.broadcasted_iota(jnp.int32, (length, length), 0)
    s_at = lax.broadcasted_iota(jnp.int32, (length, length), 1)
    count = rows_ref[DOC : DOC + 8]
    count_col = count.T[:, :1]
    far = jnp.where((t_at >= s_at) & (count_col == count[:1]), 0.0, -jnp.inf)
    lanes = lax.broadcasted_iota(jnp.int32, (length, 128), 1)

    def group(i, carry):
        g = start + i
        x_n, dy_n, b_n, c_n = (
            ref[pl.ds(g, length, stride=stride), :] for ref in (xs, ys, bs, cs)
        )
        b_t, c_t = b_n.T.astype(BF16), c_n.T.astype(BF16)
        c_n, dy_n, x_t = c_n.astype(BF16), dy_n.astype(BF16), x_n.T.astype(BF16)
        bt_ref[i] = b_t
        ct_ref[i] = c_t
        xt_ref[i] = x_t
        dyt_ref[i] = dy_n.T
        scores = dot(c_n, b_t)
        cum = jnp.concatenate(
            [rows_ref[row_of(CUM, g, 0), :], rows_ref[row_of(CUM, g, 1), :]]
            + [jnp.zeros((6, length), F32)],
            axis=0,
        )
        cum_col = cum.T
        score_grad = None
        for h in range(2):
            part = slice(h * P_SIZE, (h + 1) * P_SIZE)
            dt = rows_ref[row_of(DT, g, h), :]
            weight = jnp.exp(cum_col[:, h : h + 1] - cum[h : h + 1] + far) * dt
            high, low = split(scores * weight)
            x_h = xt_ref[i, part, :]
            dy_h = dyt_ref[i, part, :]
            yt_ref[i, part, :] = dot(x_h, high, NT) + dot(x_h, low, NT)
            dxt_ref[i, part, :] = dot(dy_h, high) + dot(dy_h, low)
            mine = (lanes < P_SIZE) if h == 0 else (lanes >= P_SIZE)
            mixing_grad = dot(jnp.where(mine, dy_n, jnp.zeros_like(dy_n)), x_t)
            score_grad = mixing_grad * weight if h == 0 else score_grad + mixing_grad * weight
        high, low = split(score_grad)
        dct_ref[i] = dot(b_t, high, NT) + dot(b_t, low, NT)
        dbt_ref[i] = dot(c_t, high) + dot(c_t, low)
        return carry

    lax.fori_loop(0, groups, group, 0)


def group_grad_kernel(
    ends_mine, ends_other, sums_mine, sums_other, rows_ref,
    xt_ref, dyt_ref, dct_ref, dbt_ref,
    own_ref, first1_ref, first3_ref, last1_ref, last3_ref, states_ref,
):
    groups, _, _ = xt_ref.shape
    owned = groups // 4
    me = lax.axis_index("mp")
    refs = (ends_mine, ends_other, sums_mine, sums_other)
    for k, (ref, place) in enumerate((
        (own_ref, 0), (own_ref, 2), (last1_ref, 0), (last1_ref, 2),
        (first1_ref, 0), (first3_ref, 0), (last3_ref, 0), (last3_ref, 2),
    )):
        g = lax.bitwise_xor(me, k // owned) * owned + k % owned
        for which, (at, vals_ref, weights, base_ref) in enumerate((
            (0, dyt_ref, ENTRY, dct_ref),
            (P_SIZE, xt_ref, TAIL, dbt_ref),
        )):
            total = base_ref[g]
            for h, state in enumerate(states_of(refs, g, groups, at)):
                states_ref[2 * g + h, at : at + P_SIZE] = state
                high, low = split(state)
                vals = vals_ref[g, h * P_SIZE : (h + 1) * P_SIZE, :]
                grad = dot(
                    jnp.concatenate([high, low], axis=0),
                    jnp.concatenate([vals, vals], axis=0),
                    TN,
                )
                total = total + grad * rows_ref[row_of(weights, g, h), :]
            ref[place + which] = total


def relay_kernel(part1_ref, part3_ref, got3_ref, got1_ref, out1_ref, out3_ref):
    out1_ref[...] = part1_ref[...] + got3_ref[...]
    out3_ref[...] = part3_ref[...] + got1_ref[...]


def finish_kernel(
    states_ref, rows_ref, xt_ref, dyt_ref, bt_ref, ct_ref, yt_ref, dxt_ref,
    rate_ref, gain_ref, order_ref,
    out_ref, dx_ref, raw_grad_ref, stats_ref,
    through, back, skip, bound,
):
    groups, _, length = xt_ref.shape
    pairs = 2 * groups
    both_heads = lax.broadcasted_iota(jnp.int32, (128, length), 0) < P_SIZE

    def group(g):
        x_t, dy_t = xt_ref[g].astype(F32), dyt_ref[g].astype(F32)
        states = [states_ref[2 * g + h, :P_SIZE] for h in range(2)]
        adjoints = [states_ref[2 * g + h, P_SIZE:] for h in range(2)]

        def entering(state, other):
            high, low = split(jnp.concatenate(state, axis=0))
            return dot(
                jnp.concatenate([high, low], axis=1), jnp.concatenate([other, other], axis=0)
            )

        y_t = yt_ref[g] + entering(states, ct_ref[g]) * two_heads(rows_ref, ENTRY, g, length)
        dx_far = entering(adjoints, bt_ref[g]) * two_heads(rows_ref, TAIL, g, length)
        dx_t = dxt_ref[g] + dx_far
        gain = jnp.where(both_heads, gain_ref[0, g], gain_ref[1, g])
        out_ref[g] = (y_t + gain * x_t).astype(BF16)
        dx_ref[g] = (dx_t + gain * dy_t).astype(BF16)
        forward, backward = dy_t * y_t, x_t * dx_t
        direct, far = dy_t * x_t, x_t * dx_far
        for h in range(2):
            part = slice(h * P_SIZE, (h + 1) * P_SIZE)
            at = row_of(0, g, h)
            through[at, :] = jnp.sum(forward[part], axis=0, keepdims=True)
            back[at, :] = jnp.sum(backward[part], axis=0, keepdims=True)
            skip[at, :] = jnp.sum(direct[part], axis=0, keepdims=True)
            meet = jnp.sum(states[h] * adjoints[h], axis=0, keepdims=True)
            passed = rows_ref[row_of(ENTRY, g, h), :][:, length - 1 :]
            arrive = jnp.sum(far[part], axis=0, keepdims=True)
            bound[at, :] = arrive + jnp.concatenate(
                [meet * passed, jnp.zeros((1, length - N), F32)], axis=1
            )

    for g in range(groups):
        group(g)
    dt = rows_ref[DT : DT + 16]
    rate = jnp.exp(pair_rows(rate_ref, pairs, length))
    before = lax.broadcasted_iota(jnp.int32, (length, length), 0)
    after = lax.broadcasted_iota(jnp.int32, (length, length), 1)
    since = jnp.where(before >= after, 1.0, 0.0).astype(F32)
    decay_grad = exact_dot(through[...] - back[...], since)
    decay_grad = decay_grad + jnp.sum(bound[...], axis=1, keepdims=True)
    raw_grad = (back[...] / dt - rate * decay_grad) * rows_ref[SIG : SIG + 16]
    for g in range(groups):
        raw_grad_ref[g] = jnp.concatenate(
            [raw_grad[g : g + 1], raw_grad[groups + g : groups + g + 1]], axis=0
        )
    rate_grad = jnp.sum(decay_grad * rows_ref[LOGD : LOGD + 16], axis=1, keepdims=True)
    bias_grad = jnp.sum(raw_grad, axis=1, keepdims=True)
    gain_grad = jnp.sum(skip[...], axis=1, keepdims=True)
    lane = lax.broadcasted_iota(jnp.int32, (pairs, 128), 1)
    stats = jnp.where(
        lane == 0, rate_grad, jnp.where(lane == 1, bias_grad, jnp.where(lane == 2, gain_grad, 0.0))
    )
    stats = jnp.concatenate([stats, jnp.zeros((128 - pairs, 128), F32)], axis=0).T[:8]
    for k in range(stats_ref.shape[0]):
        stats_ref[k] = stats


def outputs_kernel(out_in_ref, dx_in_ref, out_ref, dx_ref, ys, dxs):
    groups, _, length = out_in_ref.shape

    for src, dst, final in ((out_in_ref, ys, out_ref), (dx_in_ref, dxs, dx_ref)):
        for g in range(groups):
            dst[pl.ds(g, length, stride=groups), :] = src[g].astype(F32).T
        final[...] = dst[...].reshape(length, groups, 128).astype(BF16)


def gather_kernel(own_ref, last1_ref, last3_ref, key_ref, query_ref, keys, queries):
    length = own_ref.shape[2]
    for slot in range(4):
        total = own_ref[slot] + last1_ref[slot] + last3_ref[slot]
        dst = keys if slot % 2 else queries
        dst[pl.ds(slot // 2, length, stride=2), :] = total.T
    key_ref[...] = keys[...].reshape(key_ref.shape).astype(BF16)
    query_ref[...] = queries[...].reshape(query_ref.shape).astype(BF16)


def row_sum_kernel(got_ref, send_ref):
    total = got_ref[0]
    for k in range(1, got_ref.shape[0]):
        total = total + got_ref[k]
    for k in range(send_ref.shape[0]):
        send_ref[k] = total


def final_sum_kernel(got_ref, rate_ref, bias_ref, gain_ref):
    total = got_ref[0]
    for k in range(1, got_ref.shape[0]):
        total = total + got_ref[k]
    groups = rate_ref.shape[1]
    for k, ref in enumerate((rate_ref, bias_ref, gain_ref)):
        for h in range(2):
            ref[h : h + 1, :] = total[k : k + 1, h * groups : (h + 1) * groups]


def call(kernel, out, scratch=(), smem=(), hbm=(), flops=10**9, moved=4 << 20, vmem=24,
         out_specs=None, update=0):
    def run(*args):
        old = len(args) - update
        spaces = [
            pltpu.SMEM if i in smem else pl.ANY if i in hbm or i >= old else pltpu.VMEM
            for i in range(len(args))
        ]
        return pl.pallas_call(
            kernel,
            grid=(1,) if out_specs else (),
            out_shape=out,
            in_specs=[pl.BlockSpec(memory_space=space) for space in spaces],
            out_specs=out_specs
            or jax.tree.map(lambda _: pl.BlockSpec(memory_space=pltpu.VMEM), out),
            input_output_aliases={old + k: k for k in range(update)},
            scratch_shapes=list(scratch),
            cost_estimate=pl.CostEstimate(flops=flops, bytes_accessed=moved, transcendentals=0),
            compiler_params=pltpu.CompilerParams(vmem_limit_bytes=vmem << 20),
        )(*args)

    return run


def local(
    features, key_projection, query_proj, step_raw, doc_starts, log_rate, step_bias, skip_gain,
    out_grad,
):
    _, length, groups, _ = features.shape
    pairs = 2 * groups
    half = groups // 2
    shards, owners = lax.axis_size("seq"), lax.axis_size("mp")
    shape = jax.ShapeDtypeStruct
    flat = pltpu.VMEM((length * groups, 128), F32)
    per_pair = pltpu.VMEM((pairs, length), F32)
    summary = shape((groups, 2 * P_SIZE + 8, N), F32)
    entering = shape((groups, 2 * P_SIZE, N), F32)
    rate, bias, gain = log_rate.T, step_bias.T, skip_gain.T
    partner = [(i, i ^ 1) for i in range(shards)]
    cores = [list(range(c, shards, 2)) for c in range(2)]

    def to_chips(a):
        return lax.all_to_all(a, "seq", 0, 0, axis_index_groups=cores, tiled=True)

    keep, give, rows = call(
        summary_kernel,
        (summary, summary, shape((ROWS, length), F32)),
        scratch=[flat] * 4 + [pltpu.VMEM((length, groups, 128), BF16)] * 4
        + [pltpu.VMEM((groups, 2, length), F32), pltpu.VMEM((1, length), jnp.int32)]
        + [pltpu.SMEM((2, groups), F32)] * 2 + [pltpu.SemaphoreType.DMA((8,))],
        hbm=range(8), vmem=62,
    )(features[0], out_grad[0], key_projection[0], query_proj[0],
      step_raw[0].transpose(1, 2, 0), doc_starts, rate, bias)
    got = lax.ppermute(give, "seq", partner)
    chip = call(chip_kernel, summary)(keep, got)
    scanned = call(scan_kernel, entering)(to_chips(chip))
    ends = to_chips(scanned)
    ends_other = lax.ppermute(ends, "seq", partner)
    got_rest = lax.ppermute(keep, "seq", partner)
    full, wide = shape((groups, 128, length), F32), shape((groups, 128, length), BF16)
    within = ()
    for start in (0, half):
        block = pl.BlockSpec((half, 128, length), functools.partial(lambda at, _: (at, 0, 0), start // half))
        within = call(
            functools.partial(within_kernel, start), (full,) * 4 + (wide,) * 4,
            scratch=[flat] * 4, flops=10**10, vmem=60, out_specs=(block,) * 8, update=len(within),
        )(features[0], out_grad[0], key_projection[0], query_proj[0], rows, *within)
    y_in, dx_in, dc_in, db_in, x_t, dy_t, b_t, c_t = within
    owned = groups // owners
    part, half_part = shape((2 * owned, 128, length), F32), shape((owned, 128, length), F32)
    own, first1, first3, last1, last3, states = call(
        group_grad_kernel,
        (part, half_part, half_part, part, part, shape((pairs, 2 * P_SIZE, N), F32)),
        vmem=60,
    )(ends, ends_other, got, got_rest, rows, x_t, dy_t, dc_in, db_in)

    def to_neighbour(a, k):
        return lax.ppermute(a, "mp", [(i, i ^ k) for i in range(owners)])

    got1, got3 = to_neighbour(first1, 1), to_neighbour(first3, 3)
    mixed, dx, raw_grad, stats = call(
        finish_kernel,
        (wide, wide, shape((groups, 2, length), F32), shape((lax.axis_size("dp"), 8, 128), F32)),
        scratch=[per_pair, per_pair, per_pair, per_pair], smem=(8, 9), hbm=(10,), vmem=60,
    )(states, rows, x_t, dy_t, b_t, c_t, y_in, dx_in, rate, gain, own)
    stats = lax.all_to_all(stats, "dp", 0, 0, tiled=True)
    mixed, dx = call(
        outputs_kernel, (shape((length, groups, 128), BF16),) * 2, scratch=[flat, flat], vmem=24
    )(mixed, dx)
    stats = call(row_sum_kernel, shape((shards, 8, 128), F32), vmem=2)(stats)
    low = pl.BlockSpec((owned, 128, length), lambda _: (0, 0, 0))
    high = pl.BlockSpec((owned, 128, length), lambda _: (1, 0, 0))
    last1, last3 = pl.pallas_call(
        relay_kernel,
        name="relay",
        grid=(1,),
        out_shape=(part, part),
        in_specs=(high, low, low, low),
        out_specs=(high, low),
        input_output_aliases={0: 0, 1: 1},
        cost_estimate=pl.CostEstimate(flops=10**6, bytes_accessed=3 << 19, transcendentals=0),
        compiler_params=pltpu.CompilerParams(vmem_limit_bytes=60 << 20),
    )(last1, last3, got3, got1)
    last1, last3 = to_neighbour(last1, 1), to_neighbour(last3, 3)
    stats = lax.all_to_all(stats, "seq", 0, 0, tiled=True)
    sums = call(final_sum_kernel, (shape((2, groups), F32),) * 3, vmem=2)(stats)
    out_grads = shape((length, owned, 128), BF16)
    key_grad, query_grad = call(
        gather_kernel, (out_grads, out_grads),
        scratch=[pltpu.VMEM((length * owned, 128), F32)] * 2, vmem=24,
    )(own, last1, last3)
    return (
        mixed[None],
        dx[None],
        key_grad[None],
        query_grad[None],
        raw_grad.transpose(2, 0, 1)[None],
        *(total.T for total in sums),
    )


def solution(mesh):
    return jax.shard_map(
        local,
        mesh=mesh,
        in_specs=(
            P("dp", "seq", None, "mp"),
            P("dp", "seq", None, None),
            P("dp", "seq", None, None),
            P("dp", "seq", None, "mp"),
            P("dp", "seq"),
            P(None, "mp"),
            P(None, "mp"),
            P(None, "mp"),
            P("dp", "seq", None, "mp"),
        ),
        out_specs=(
            P("dp", "seq", None, "mp"),
            P("dp", "seq", None, "mp"),
            P("dp", "seq", "mp", None),
            P("dp", "seq", "mp", None),
            P("dp", "seq", None, "mp"),
            P(None, "mp"),
            P(None, "mp"),
            P(None, "mp"),
        ),
        check_vma=False,
    )
```

```python
import functools

import jax
import jax.numpy as jnp
from jax import lax
from jax.experimental import pallas as pl
from jax.experimental.pallas import tpu as pltpu
from jax.sharding import PartitionSpec as P


P_SIZE = 64
N = 128
F32 = jnp.float32
BF16 = jnp.bfloat16
NN = (((1,), (0,)), ((), ()))
NT = (((1,), (1,)), ((), ()))
TN = (((0,), (0,)), ((), ()))


def dot(a, b, dims=NN):
    return lax.dot_general(a, b, dims, preferred_element_type=F32)


def split(a):
    high = a.astype(BF16)
    return high, (a - high.astype(F32)).astype(BF16)


def exact_dot(a, b):
    return lax.dot_general(
        a, b, NN, precision=lax.Precision.HIGHEST, preferred_element_type=F32
    )


def softplus(v):
    u = jnp.exp(-jnp.abs(v))
    series = u * (1.0 + u * (-1.0 / 2 + u * (1.0 / 3 + u * (-1.0 / 4 + u * (1.0 / 5)))))
    return jnp.maximum(v, 0.0) + jnp.where(u < 0.03, series, jnp.log(1.0 + u))


def pair_rows(ref, pairs, length):
    half = pairs // 2
    rows = [jnp.full((1, length), ref[j // half, j % half], F32) for j in range(pairs)]
    return jnp.concatenate(rows, axis=0)


def row_of(base, g, h):
    return pl.ds(base + 8 * h + g, 1)


def two_heads(rows_ref, base, g, length):
    top, low = rows_ref[row_of(base, g, 0), :], rows_ref[row_of(base, g, 1), :]
    return jnp.concatenate(
        [jnp.broadcast_to(top, (P_SIZE, length)), jnp.broadcast_to(low, (P_SIZE, length))], axis=0
    )


CUM, DT, ENTRY, TAIL, SIG, LOGD, DOC = 0, 16, 32, 48, 64, 80, 96
ROWS = 104


def summary_kernel(
    x_hbm, dy_hbm, b_hbm, c_hbm, raw_hbm, doc_hbm, rate_hbm, bias_hbm,
    keep_ref, give_ref, rows_ref,
    xs, ys, bs, cs, x_in, dy_in, b_in, c_in, raw_ref, doc_ref, rate_ref, bias_ref, sems,
):
    length, groups, _ = x_hbm.shape
    loads = [
        pltpu.make_async_copy(src, dst, sems.at[k])
        for k, (src, dst) in enumerate((
            (raw_hbm, raw_ref), (doc_hbm, doc_ref), (rate_hbm, rate_ref), (bias_hbm, bias_ref),
            (x_hbm, x_in), (dy_hbm, dy_in), (b_hbm, b_in), (c_hbm, c_in),
        ))
    ]
    for load in loads:
        load.start()
    for load in loads[:4]:
        load.wait()
    pairs = 2 * groups
    core = core_of_chip()
    raw = jnp.concatenate(
        [raw_ref[g, h : h + 1, :] for h in range(2) for g in range(groups)], axis=0
    )
    shifted = raw + pair_rows(bias_ref, pairs, length)
    dt = softplus(shifted)
    log_decay = -dt * jnp.exp(pair_rows(rate_ref, pairs, length))
    docs = jnp.broadcast_to(doc_ref[...].astype(F32), (8, length))
    before = lax.broadcasted_iota(jnp.int32, (length, length), 0)
    after = lax.broadcasted_iota(jnp.int32, (length, length), 1)
    upto = jnp.where(before <= after, 1.0, 0.0).astype(F32)
    sums = exact_dot(jnp.concatenate([log_decay, docs], axis=0), upto)
    cum = sums[:pairs]
    count = sums[pairs : pairs + 1]
    last = cum[:, length - 1 :]
    last_count = count[:, length - 1 :]
    entry = jnp.where(count == 0.0, jnp.exp(cum), 0.0)
    tail = jnp.where(count == last_count, jnp.exp(last - cum), 0.0) * dt
    rows_ref[CUM : CUM + 16] = cum
    rows_ref[DT : DT + 16] = dt
    rows_ref[ENTRY : ENTRY + 16] = entry
    rows_ref[TAIL : TAIL + 16] = tail
    rows_ref[SIG : SIG + 16] = 1.0 / (1.0 + jnp.exp(-shifted))
    rows_ref[LOGD : LOGD + 16] = log_decay
    rows_ref[DOC : DOC + 8] = jnp.broadcast_to(count, (8, length))
    for load, src, dst in zip(loads[4:], (x_in, dy_in, b_in, c_in), (xs, ys, bs, cs)):
        load.wait()
        dst[...] = src[...].astype(F32).reshape(length * groups, 128)

    def totals_of(g):
        x_t = xs[pl.ds(g, length, stride=groups), :].T
        dy_t = ys[pl.ds(g, length, stride=groups), :].T
        b_n = bs[pl.ds(g, length, stride=groups), :].astype(BF16)
        c_n = cs[pl.ds(g, length, stride=groups), :].astype(BF16)
        totals = []
        for vals, weights, other in ((x_t, TAIL, b_n), (dy_t, ENTRY, c_n)):
            high, low = split(vals * two_heads(rows_ref, weights, g, length))
            both = dot(jnp.concatenate([high, low], axis=0), other)
            totals.append(both[:128] + both[128:])
        return totals

    half = groups // 2
    passed = entry[:, length - 1 :]
    for i in range(half):
        low, high = totals_of(i), totals_of(half + i)
        for h in range(2):
            part = slice(h * P_SIZE, (h + 1) * P_SIZE)
            for at, a, b in zip((0, P_SIZE), low, high):
                keep_ref[2 * i + h, at : at + P_SIZE] = jnp.where(core == 0, a[part], b[part])
                give_ref[2 * i + h, at : at + P_SIZE] = jnp.where(core == 0, b[part], a[part])
            a = jnp.broadcast_to(passed[groups * h + i : groups * h + i + 1], (8, N))
            b = jnp.broadcast_to(passed[groups * h + half + i : groups * h + half + i + 1], (8, N))
            keep_ref[2 * i + h, 2 * P_SIZE :] = jnp.where(core == 0, a, b)
            give_ref[2 * i + h, 2 * P_SIZE :] = jnp.where(core == 0, b, a)


def core_of_chip():
    return lax.rem(lax.axis_index("seq"), 2)


def state_of(ref, k):
    return ref[k, :P_SIZE]


def adjoint_of(ref, k):
    return ref[k, P_SIZE : 2 * P_SIZE]


def passed_of(ref, k):
    return ref[k, 2 * P_SIZE : 2 * P_SIZE + 1, :]


def chip_kernel(keep_ref, got_ref, chip_ref):
    def join(first, second):
        for k in range(chip_ref.shape[0]):
            chip_ref[k, :P_SIZE] = passed_of(second, k) * state_of(first, k) + state_of(second, k)
            chip_ref[k, P_SIZE : 2 * P_SIZE] = adjoint_of(first, k) + passed_of(
                first, k
            ) * adjoint_of(second, k)
            chip_ref[k, 2 * P_SIZE :] = first[k, 2 * P_SIZE :] * second[k, 2 * P_SIZE :]

    core = core_of_chip()
    pl.when(core == 0)(lambda: join(keep_ref, got_ref))
    pl.when(core == 1)(lambda: join(got_ref, keep_ref))


def scan_kernel(recv_ref, send_ref):
    chips = recv_ref.shape[0]
    state = jnp.zeros((P_SIZE, N), F32)
    for k in range(chips):
        send_ref[k, :P_SIZE] = state
        if k < chips - 1:
            state = passed_of(recv_ref, k) * state + state_of(recv_ref, k)
    state = jnp.zeros((P_SIZE, N), F32)
    for k in reversed(range(chips)):
        send_ref[k, P_SIZE:] = state
        if k > 0:
            state = passed_of(recv_ref, k) * state + adjoint_of(recv_ref, k)


def states_of(refs, g, groups, at):
    core = core_of_chip()
    mine = g // (groups // 2) == core
    through = core == (1 if at == 0 else 0)
    slot = 2 * lax.rem(g, groups // 2)
    ends_mine, ends_other, sums_mine, sums_other = refs
    part = slice(at, at + P_SIZE)
    states = []
    for k in (slot, slot + 1):
        end = jnp.where(mine, ends_mine[k, part], ends_other[k, part])
        summary = jnp.where(mine, sums_mine[k, part], sums_other[k, part])
        passed = jnp.where(mine, passed_of(sums_mine, k), passed_of(sums_other, k))
        states.append(jnp.where(through, passed * end + summary, end))
    return states


def within_kernel(
    start,
    x_ref, dy_ref, b_ref, c_ref, rows_ref,
    *rest,
):
    yt_ref, dxt_ref, dct_ref, dbt_ref, xt_ref, dyt_ref, bt_ref, ct_ref, xs, ys, bs, cs = rest[-12:]
    groups, _, length = yt_ref.shape
    stride = x_ref.shape[1]
    for src, dst in ((x_ref, xs), (dy_ref, ys), (b_ref, bs), (c_ref, cs)):
        dst[...] = src[...].astype(F32).reshape(length * stride, 128)
    t_at = lax.broadcasted_iota(jnp.int32, (length, length), 0)
    s_at = lax.broadcasted_iota(jnp.int32, (length, length), 1)
    count = rows_ref[DOC : DOC + 8]
    count_col = count.T[:, :1]
    far = jnp.where((t_at >= s_at) & (count_col == count[:1]), 0.0, -jnp.inf)
    lanes = lax.broadcasted_iota(jnp.int32, (length, 128), 1)

    def group(i, carry):
        g = start + i
        x_n, dy_n, b_n, c_n = (
            ref[pl.ds(g, length, stride=stride), :] for ref in (xs, ys, bs, cs)
        )
        b_t, c_t = b_n.T.astype(BF16), c_n.T.astype(BF16)
        c_n, dy_n, x_t = c_n.astype(BF16), dy_n.astype(BF16), x_n.T.astype(BF16)
        bt_ref[i] = b_t
        ct_ref[i] = c_t
        xt_ref[i] = x_t
        dyt_ref[i] = dy_n.T
        scores = dot(c_n, b_t)
        cum = jnp.concatenate(
            [rows_ref[row_of(CUM, g, 0), :], rows_ref[row_of(CUM, g, 1), :]]
            + [jnp.zeros((6, length), F32)],
            axis=0,
        )
        cum_col = cum.T
        score_grad = None
        for h in range(2):
            part = slice(h * P_SIZE, (h + 1) * P_SIZE)
            dt = rows_ref[row_of(DT, g, h), :]
            weight = jnp.exp(cum_col[:, h : h + 1] - cum[h : h + 1] + far) * dt
            high, low = split(scores * weight)
            x_h = xt_ref[i, part, :]
            dy_h = dyt_ref[i, part, :]
            yt_ref[i, part, :] = dot(x_h, high, NT) + dot(x_h, low, NT)
            dxt_ref[i, part, :] = dot(dy_h, high) + dot(dy_h, low)
            mine = (lanes < P_SIZE) if h == 0 else (lanes >= P_SIZE)
            mixing_grad = dot(jnp.where(mine, dy_n, jnp.zeros_like(dy_n)), x_t)
            score_grad = mixing_grad * weight if h == 0 else score_grad + mixing_grad * weight
        high, low = split(score_grad)
        dct_ref[i] = dot(b_t, high, NT) + dot(b_t, low, NT)
        dbt_ref[i] = dot(c_t, high) + dot(c_t, low)
        return carry

    lax.fori_loop(0, groups, group, 0)


def group_grad_kernel(
    ends_mine, ends_other, sums_mine, sums_other, rows_ref,
    xt_ref, dyt_ref, dct_ref, dbt_ref,
    own_ref, first1_ref, first3_ref, last1_ref, last3_ref, states_ref,
):
    groups, _, _ = xt_ref.shape
    owned = groups // 4
    me = lax.axis_index("mp")
    refs = (ends_mine, ends_other, sums_mine, sums_other)
    for k, (ref, place) in enumerate((
        (own_ref, 0), (own_ref, 2), (last1_ref, 0), (last1_ref, 2),
        (first1_ref, 0), (first3_ref, 0), (last3_ref, 0), (last3_ref, 2),
    )):
        g = lax.bitwise_xor(me, k // owned) * owned + k % owned
        for which, (at, vals_ref, weights, base_ref) in enumerate((
            (0, dyt_ref, ENTRY, dct_ref),
            (P_SIZE, xt_ref, TAIL, dbt_ref),
        )):
            total = base_ref[g]
            for h, state in enumerate(states_of(refs, g, groups, at)):
                states_ref[2 * g + h, at : at + P_SIZE] = state
                high, low = split(state)
                vals = vals_ref[g, h * P_SIZE : (h + 1) * P_SIZE, :]
                grad = dot(
                    jnp.concatenate([high, low], axis=0),
                    jnp.concatenate([vals, vals], axis=0),
                    TN,
                )
                total = total + grad * rows_ref[row_of(weights, g, h), :]
            ref[place + which] = total


def relay_kernel(part1_ref, part3_ref, got3_ref, got1_ref, out1_ref, out3_ref):
    out1_ref[...] = part1_ref[...] + got3_ref[...]
    out3_ref[...] = part3_ref[...] + got1_ref[...]


def finish_kernel(
    states_ref, rows_ref, xt_ref, dyt_ref, bt_ref, ct_ref, yt_ref, dxt_ref,
    rate_ref, gain_ref, order_ref,
    out_ref, dx_ref, raw_grad_ref, stats_ref,
    through, back, skip, bound,
):
    groups, _, length = xt_ref.shape
    pairs = 2 * groups
    both_heads = lax.broadcasted_iota(jnp.int32, (128, length), 0) < P_SIZE

    def group(g):
        x_t, dy_t = xt_ref[g].astype(F32), dyt_ref[g].astype(F32)
        states = [states_ref[2 * g + h, :P_SIZE] for h in range(2)]
        adjoints = [states_ref[2 * g + h, P_SIZE:] for h in range(2)]

        def entering(state, other):
            high, low = split(jnp.concatenate(state, axis=0))
            return dot(
                jnp.concatenate([high, low], axis=1), jnp.concatenate([other, other], axis=0)
            )

        y_t = yt_ref[g] + entering(states, ct_ref[g]) * two_heads(rows_ref, ENTRY, g, length)
        dx_far = entering(adjoints, bt_ref[g]) * two_heads(rows_ref, TAIL, g, length)
        dx_t = dxt_ref[g] + dx_far
        gain = jnp.where(both_heads, gain_ref[0, g], gain_ref[1, g])
        out_ref[g] = (y_t + gain * x_t).astype(BF16)
        dx_ref[g] = (dx_t + gain * dy_t).astype(BF16)
        forward, backward = dy_t * y_t, x_t * dx_t
        direct, far = dy_t * x_t, x_t * dx_far
        for h in range(2):
            part = slice(h * P_SIZE, (h + 1) * P_SIZE)
            at = row_of(0, g, h)
            through[at, :] = jnp.sum(forward[part], axis=0, keepdims=True)
            back[at, :] = jnp.sum(backward[part], axis=0, keepdims=True)
            skip[at, :] = jnp.sum(direct[part], axis=0, keepdims=True)
            meet = jnp.sum(states[h] * adjoints[h], axis=0, keepdims=True)
            passed = rows_ref[row_of(ENTRY, g, h), :][:, length - 1 :]
            arrive = jnp.sum(far[part], axis=0, keepdims=True)
            bound[at, :] = arrive + jnp.concatenate(
                [meet * passed, jnp.zeros((1, length - N), F32)], axis=1
            )

    for g in range(groups):
        group(g)
    dt = rows_ref[DT : DT + 16]
    rate = jnp.exp(pair_rows(rate_ref, pairs, length))
    before = lax.broadcasted_iota(jnp.int32, (length, length), 0)
    after = lax.broadcasted_iota(jnp.int32, (length, length), 1)
    since = jnp.where(before >= after, 1.0, 0.0).astype(F32)
    decay_grad = exact_dot(through[...] - back[...], since)
    decay_grad = decay_grad + jnp.sum(bound[...], axis=1, keepdims=True)
    raw_grad = (back[...] / dt - rate * decay_grad) * rows_ref[SIG : SIG + 16]
    for g in range(groups):
        raw_grad_ref[g] = jnp.concatenate(
            [raw_grad[g : g + 1], raw_grad[groups + g : groups + g + 1]], axis=0
        )
    rate_grad = jnp.sum(decay_grad * rows_ref[LOGD : LOGD + 16], axis=1, keepdims=True)
    bias_grad = jnp.sum(raw_grad, axis=1, keepdims=True)
    gain_grad = jnp.sum(skip[...], axis=1, keepdims=True)
    lane = lax.broadcasted_iota(jnp.int32, (pairs, 128), 1)
    stats = jnp.where(
        lane == 0, rate_grad, jnp.where(lane == 1, bias_grad, jnp.where(lane == 2, gain_grad, 0.0))
    )
    stats = jnp.concatenate([stats, jnp.zeros((128 - pairs, 128), F32)], axis=0).T[:8]
    for k in range(stats_ref.shape[0]):
        stats_ref[k] = stats


def outputs_kernel(out_in_ref, dx_in_ref, out_ref, dx_ref, ys, dxs):
    groups, _, length = out_in_ref.shape

    for src, dst, final in ((out_in_ref, ys, out_ref), (dx_in_ref, dxs, dx_ref)):
        for g in range(groups):
            dst[pl.ds(g, length, stride=groups), :] = src[g].astype(F32).T
        final[...] = dst[...].reshape(length, groups, 128).astype(BF16)


def gather_kernel(own_ref, last1_ref, last3_ref, key_ref, query_ref, keys, queries):
    length = own_ref.shape[2]
    for slot in range(4):
        total = own_ref[slot] + last1_ref[slot] + last3_ref[slot]
        dst = keys if slot % 2 else queries
        dst[pl.ds(slot // 2, length, stride=2), :] = total.T
    key_ref[...] = keys[...].reshape(key_ref.shape).astype(BF16)
    query_ref[...] = queries[...].reshape(query_ref.shape).astype(BF16)


def row_sum_kernel(got_ref, send_ref):
    total = got_ref[0]
    for k in range(1, got_ref.shape[0]):
        total = total + got_ref[k]
    for k in range(send_ref.shape[0]):
        send_ref[k] = total


def final_sum_kernel(got_ref, rate_ref, bias_ref, gain_ref):
    total = got_ref[0]
    for k in range(1, got_ref.shape[0]):
        total = total + got_ref[k]
    groups = rate_ref.shape[1]
    for k, ref in enumerate((rate_ref, bias_ref, gain_ref)):
        for h in range(2):
            ref[h : h + 1, :] = total[k : k + 1, h * groups : (h + 1) * groups]


def call(kernel, out, scratch=(), smem=(), hbm=(), flops=10**9, moved=4 << 20, vmem=24,
         out_specs=None, update=0):
    def run(*args):
        old = len(args) - update
        spaces = [
            pltpu.SMEM if i in smem else pl.ANY if i in hbm or i >= old else pltpu.VMEM
            for i in range(len(args))
        ]
        return pl.pallas_call(
            kernel,
            grid=(1,) if out_specs else (),
            out_shape=out,
            in_specs=[pl.BlockSpec(memory_space=space) for space in spaces],
            out_specs=out_specs
            or jax.tree.map(lambda _: pl.BlockSpec(memory_space=pltpu.VMEM), out),
            input_output_aliases={old + k: k for k in range(update)},
            scratch_shapes=list(scratch),
            cost_estimate=pl.CostEstimate(flops=flops, bytes_accessed=moved, transcendentals=0),
            compiler_params=pltpu.CompilerParams(vmem_limit_bytes=vmem << 20),
        )(*args)

    return run


def local(
    features, key_projection, query_proj, step_raw, doc_starts, log_rate, step_bias, skip_gain,
    out_grad,
):
    _, length, groups, _ = features.shape
    pairs = 2 * groups
    half = groups // 2
    shards, owners = lax.axis_size("seq"), lax.axis_size("mp")
    shape = jax.ShapeDtypeStruct
    flat = pltpu.VMEM((length * groups, 128), F32)
    per_pair = pltpu.VMEM((pairs, length), F32)
    summary = shape((groups, 2 * P_SIZE + 8, N), F32)
    entering = shape((groups, 2 * P_SIZE, N), F32)
    rate, bias, gain = log_rate.T, step_bias.T, skip_gain.T
    partner = [(i, i ^ 1) for i in range(shards)]
    cores = [list(range(c, shards, 2)) for c in range(2)]

    def to_chips(a):
        return lax.all_to_all(a, "seq", 0, 0, axis_index_groups=cores, tiled=True)

    keep, give, rows = call(
        summary_kernel,
        (summary, summary, shape((ROWS, length), F32)),
        scratch=[flat] * 4 + [pltpu.VMEM((length, groups, 128), BF16)] * 4
        + [pltpu.VMEM((groups, 2, length), F32), pltpu.VMEM((1, length), jnp.int32)]
        + [pltpu.SMEM((2, groups), F32)] * 2 + [pltpu.SemaphoreType.DMA((8,))],
        hbm=range(8), vmem=62,
    )(features[0], out_grad[0], key_projection[0], query_proj[0],
      step_raw[0].transpose(1, 2, 0), doc_starts, rate, bias)
    got = lax.ppermute(give, "seq", partner)
    chip = call(chip_kernel, summary)(keep, got)
    scanned = call(scan_kernel, entering)(to_chips(chip))
    ends = to_chips(scanned)
    ends_other = lax.ppermute(ends, "seq", partner)
    got_rest = lax.ppermute(keep, "seq", partner)
    full, wide = shape((groups, 128, length), F32), shape((groups, 128, length), BF16)
    within = ()
    for start in (0, half):
        block = pl.BlockSpec((half, 128, length), functools.partial(lambda at, _: (at, 0, 0), start // half))
        within = call(
            functools.partial(within_kernel, start), (full,) * 4 + (wide,) * 4,
            scratch=[flat] * 4, flops=10**10, vmem=60, out_specs=(block,) * 8, update=len(within),
        )(features[0], out_grad[0], key_projection[0], query_proj[0], rows, *within)
    y_in, dx_in, dc_in, db_in, x_t, dy_t, b_t, c_t = within
    owned = groups // owners
    part, half_part = shape((2 * owned, 128, length), F32), shape((owned, 128, length), F32)
    own, first1, first3, last1, last3, states = call(
        group_grad_kernel,
        (part, half_part, half_part, part, part, shape((pairs, 2 * P_SIZE, N), F32)),
        vmem=48,
    )(ends, ends_other, got, got_rest, rows, x_t, dy_t, dc_in, db_in)

    def to_neighbour(a, k):
        return lax.ppermute(a, "mp", [(i, i ^ k) for i in range(owners)])

    got1, got3 = to_neighbour(first1, 1), to_neighbour(first3, 3)
    mixed, dx, raw_grad, stats = call(
        finish_kernel,
        (wide, wide, shape((groups, 2, length), F32), shape((shards, 8, 128), F32)),
        scratch=[per_pair, per_pair, per_pair, per_pair], smem=(8, 9), hbm=(10,), vmem=28,
    )(states, rows, x_t, dy_t, b_t, c_t, y_in, dx_in, rate, gain, own)
    stats = lax.all_to_all(stats, "seq", 0, 0, tiled=True)
    mixed, dx = call(
        outputs_kernel, (shape((length, groups, 128), BF16),) * 2, scratch=[flat, flat], vmem=24
    )(mixed, dx)
    stats = call(row_sum_kernel, shape((lax.axis_size("dp"), 8, 128), F32), vmem=2)(stats)
    low = pl.BlockSpec((owned, 128, length), lambda _: (0, 0, 0))
    high = pl.BlockSpec((owned, 128, length), lambda _: (1, 0, 0))
    last1, last3 = pl.pallas_call(
        relay_kernel,
        name="relay",
        grid=(1,),
        out_shape=(part, part),
        in_specs=(high, low, low, low),
        out_specs=(high, low),
        input_output_aliases={0: 0, 1: 1},
        cost_estimate=pl.CostEstimate(flops=10**6, bytes_accessed=3 << 19, transcendentals=0),
        compiler_params=pltpu.CompilerParams(vmem_limit_bytes=24 << 20),
    )(last1, last3, got3, got1)
    last1, last3 = to_neighbour(last1, 1), to_neighbour(last3, 3)
    stats = lax.all_to_all(stats, "dp", 0, 0, tiled=True)
    sums = call(final_sum_kernel, (shape((2, groups), F32),) * 3, vmem=2)(stats)
    out_grads = shape((length, owned, 128), BF16)
    key_grad, query_grad = call(
        gather_kernel, (out_grads, out_grads),
        scratch=[pltpu.VMEM((length * owned, 128), F32)] * 2, vmem=24,
    )(own, last1, last3)
    return (
        mixed[None],
        dx[None],
        key_grad[None],
        query_grad[None],
        raw_grad.transpose(2, 0, 1)[None],
        *(total.T for total in sums),
    )


def solution(mesh):
    return jax.shard_map(
        local,
        mesh=mesh,
        in_specs=(
            P("dp", "seq", None, "mp"),
            P("dp", "seq", None, None),
            P("dp", "seq", None, None),
            P("dp", "seq", None, "mp"),
            P("dp", "seq"),
            P(None, "mp"),
            P(None, "mp"),
            P(None, "mp"),
            P("dp", "seq", None, "mp"),
        ),
        out_specs=(
            P("dp", "seq", None, "mp"),
            P("dp", "seq", None, "mp"),
            P("dp", "seq", "mp", None),
            P("dp", "seq", "mp", None),
            P("dp", "seq", None, "mp"),
            P(None, "mp"),
            P(None, "mp"),
            P(None, "mp"),
        ),
        check_vma=False,
    )
```
